32 devices in a mesh: row: 4 (over y, x), col: 8 (over z, core).
Axes of the slice: x: 2, y: 2, z: 4, core: 2. Of those that a mesh axis runs over, the one named last changes fastest.
Arguments:
- hist_corr: float32 [16384, 16384], P('row', 'col'), may hold values from -1 to 1
- hist_resp: float32 [16384, 16384], P('row', 'col'), may hold values from -1 to 1, as said below
- row_corr: float32 [128, 16384], P(None, 'col'), may hold values from -1 to 1
- row_resp: float32 [128, 16384], P(None, 'col'), may hold values from -1 to 1
Outputs:
- final_corr: float32 [128, 16384], P(None, 'col')
- final_resp: float32 [128, 16384], P(None, 'col')
The draws below stay inside these ranges and needn't reach their ends.
Inputs may be any that keep to these rules, and one draw needn't show every extreme that they name: hist_resp[s, u] is 0 where u > s and 1 where u == s.
All inputs are finite; a program needn't handle non-finite values.
Results may differ from the reference program's by a relative error of at most 0.00015.
Values sent between devices are 32-bit elements; how exact they have to be, the bound alone decides.
A program may use at most 128 MiB of HBM per device.

```python
import math
import jax
import jax.numpy as jnp
from jax import lax

HIST = 16384
ROWS = 128
BLOCKS = 4


def draw_hist_corr(key, part):
    base_key = jax.random.fold_in(key, 101)
    rough_part = jax.random.uniform(base_key, (HIST, HIST), jnp.float32, -1.0, 1.0)
    return rough_part


def draw_hist_resp(key, part):
    base_key = jax.random.fold_in(key, 202)
    rough_part = jax.random.uniform(base_key, (HIST, HIST), jnp.float32, -1.0, 1.0)
    time_index = jnp.arange(HIST, dtype=jnp.int32)
    later_mask = time_index[:, None] > time_index[None, :]
    diagonal_mask = time_index[:, None] == time_index[None, :]
    filled = jnp.where(diagonal_mask, jnp.float32(1.0), jnp.float32(0.0))
    return jnp.where(later_mask, rough_part, filled).astype(jnp.float32)


def draw_rows(key, salt_value):
    base_key = jax.random.fold_in(key, salt_value)
    time_grid = jnp.arange(HIST, dtype=jnp.int32).astype(jnp.float32) / HIST
    rough_part = jax.random.uniform(base_key, (ROWS, HIST), jnp.float32, -1.0, 1.0)
    return rough_part * (0.55 + 0.45 * time_grid)[None, :]


def draw_row_corr(key, part):
    return draw_rows(key, 303)


def draw_row_resp(key, part):
    return draw_rows(key, 404)


def setup_inputs(seed: int = 0) -> dict:
    splits = jax.random.split(jax.random.key(seed), 5)
    hist_corr = draw_hist_corr(jax.random.fold_in(splits[4], 71), 0)
    hist_resp = draw_hist_resp(jax.random.fold_in(splits[4], 71), 0)
    row_corr = draw_row_corr(jax.random.fold_in(splits[4], 71), 0)
    row_resp = draw_row_resp(jax.random.fold_in(splits[4], 71), 0)
    return {"hist_corr": hist_corr, "hist_resp": hist_resp, "row_corr": row_corr, "row_resp": row_resp}


step_size = 0.2
heat_reservoir_warmth = 0.6

def reference(hist_corr, hist_resp, row_corr, row_resp):
    highest = lax.Precision.HIGHEST
    integration_coefficient = 1.0 / math.sqrt(HIST)
    autocovariance_curve = row_corr
    perturbation_reaction = row_resp
    for block_index in range(BLOCKS):
        history_integrand = 3.0 * autocovariance_curve * perturbation_reaction
        slope_contribution = 1.5 * autocovariance_curve * autocovariance_curve
        norm_enforcing_scalar = heat_reservoir_warmth + integration_coefficient * lax.optimization_barrier(jnp.sum(history_integrand * autocovariance_curve + slope_contribution * perturbation_reaction, axis=1, keepdims=True))
        memory_corr = jnp.dot(history_integrand, hist_corr, precision=highest, preferred_element_type=jnp.float32)
        memory_resp = jnp.dot(history_integrand, hist_resp, precision=highest, preferred_element_type=jnp.float32)
        memory_cross = lax.dot_general(slope_contribution, hist_resp, (((1,), (1,)), ((), ())), precision=highest, preferred_element_type=jnp.float32)
        next_corr = autocovariance_curve + step_size * (integration_coefficient * (memory_corr + memory_cross) - norm_enforcing_scalar * autocovariance_curve)
        next_resp = perturbation_reaction + step_size * (integration_coefficient * memory_resp - norm_enforcing_scalar * perturbation_reaction)
        autocovariance_curve = next_corr
        perturbation_reaction = next_resp
    return (autocovariance_curve, perturbation_reaction)
```

```python
import functools
import math

import jax
import jax.numpy as jnp
from jax import lax
from jax.experimental import pallas as pl
from jax.experimental.pallas import tpu as pltpu
from jax.sharding import PartitionSpec as P

BLOCKS = 4
STEP = 0.2
WARMTH = 0.6


def plain_body(hist_corr, hist_resp, row_corr, row_resp):
    rows = lax.axis_size("row")
    span = row_corr.shape[0] // rows
    coef = 1.0 / math.sqrt(hist_corr.shape[0] * rows)
    start = lax.axis_index("row") * span
    corr = lax.dynamic_slice_in_dim(row_corr, start, span, 0)
    resp = lax.dynamic_slice_in_dim(row_resp, start, span, 0)

    def dot(a, b, dims):
        return lax.dot_general(
            a, b, (dims, ((), ())), precision=lax.Precision.HIGH, preferred_element_type=jnp.float32
        )

    for _ in range(BLOCKS):
        energy = 3.0 * corr * resp
        slope = 1.5 * corr * corr
        mult = lax.psum(jnp.sum(energy * corr + slope * resp, axis=1), "col")
        full = lax.all_gather(corr, "row", axis=0, tiled=True)
        wide = lax.all_gather(energy, "col", axis=1, tiled=True)
        energy_rows = lax.all_to_all(wide, "row", split_axis=1, concat_axis=0, tiled=True)
        part_cross = dot(1.5 * full * full, hist_resp, ((1,), (1,)))
        turned = lax.all_to_all(part_cross, "row", split_axis=0, concat_axis=1, tiled=True)
        cross = lax.psum_scatter(turned, "col", scatter_dimension=1, tiled=True)
        part_corr = dot(energy_rows, hist_corr, ((1,), (0,)))
        part_resp = dot(energy_rows, hist_resp, ((1,), (0,)))
        mem_corr = lax.psum_scatter(part_corr, "row", scatter_dimension=0, tiled=True)
        mem_resp = lax.psum_scatter(part_resp, "row", scatter_dimension=0, tiled=True)
        scalar = WARMTH + coef * mult[:, None]
        next_corr = corr + STEP * (coef * (mem_corr + cross) - scalar * corr)
        resp = resp + STEP * (coef * mem_resp - scalar * resp)
        corr = next_corr
    return (
        lax.all_gather(corr, "row", axis=0, tiled=True),
        lax.all_gather(resp, "row", axis=0, tiled=True),
    )


MESH = pl.DeviceIdType.MESH
F32 = jnp.float32


SLOTS = 3
BF16 = jnp.bfloat16


def split(x):
    hi = x.astype(BF16)
    return hi, (x - hi.astype(F32)).astype(BF16)


def block_kernel(last, coef, R, Z, hc, hr, c_prev, c_in, r_in, *refs):
    refs = list(refs)
    take = lambda n: [refs.pop(0) for _ in range(n)]
    if last:
        c_full, r_full = take(2)
    else:
        c_out, r_out, c_full = take(3)
    tiles, xp, acc, e_rows, estack, dstack = take(6)
    xbuf, xsum, xin, up, mrecv, racc, csrc, eall, mbuf = take(9)
    (tsem,) = take(1)
    xs, xr, xis, xir, ups, upr, ms, mrs, cs, crs = take(10)
    eus, eur, eds, edr, eis, eir, ps, pr, mus, mur = take(10)
    assert not refs
    T, U = c_in.shape
    M = R * T
    N = 2 * Z
    CH = tiles.shape[1]
    per = U // CH
    count = 2 * per
    r, c = lax.axis_index("row"), lax.axis_index("col")
    z = lax.div(c, 2)
    k = c - 2 * z
    partner = 2 * z + 1 - k
    rows = [lax.rem(r + d, R) for d in range(1, R)]
    cols = [lax.rem(c + d, N) for d in range(1, N)]
    low = z <= r

    def rc(src, dst, ss, rs, row, col):
        return pltpu.make_async_remote_copy(
            src_ref=src, dst_ref=dst, send_sem=ss, recv_sem=rs, device_id=(row, col), device_id_type=MESH
        )

    def at_row(q):
        return pl.ds(pl.multiple_of(q * T, T), T)

    def half(h):
        return pl.ds(pl.multiple_of(h * U, U), U)

    def x_start(i):
        side = 1 - k if i < per else k
        return pl.multiple_of(side * U + (i % per) * CH, CH)

    def tile_copy(n):
        kind, i = divmod(n, count)
        start = x_start(i) if kind == 0 else i * CH
        src = hc if kind == 1 else hr
        return pltpu.make_async_copy(src.at[pl.ds(start, CH)], tiles.at[n % SLOTS], tsem.at[n % SLOTS])

    tile_copy(0).start()
    tile_copy(1).start()

    barrier = pltpu.get_barrier_semaphore()
    for q in rows:
        pl.semaphore_signal(barrier, inc=1, device_id=(q, c), device_id_type=MESH)
    for q in cols:
        pl.semaphore_signal(barrier, inc=1, device_id=(r, q), device_id_type=MESH)

    energy = 3.0 * c_in[...] * r_in[...]
    eall[z] = energy
    terms = energy * c_in[...] + 1.5 * c_in[...] * c_in[...] * r_in[...]
    part = terms[:, :128]
    for i in range(1, U // 128):
        part = part + terms[:, i * 128 : (i + 1) * 128]
    mbuf[c] = part
    pl.semaphore_wait(barrier, R - 1 + N - 1)

    def flow(p, step):
        ss, rs = (eus, eur) if step > 0 else (eds, edr)
        return rc(eall.at[p], eall.at[p], ss.at[p], rs.at[p], r, c + step)

    def inplane(d, p):
        return rc(eall.at[p], e_rows.at[at_row(r), half(k)], eis.at[d], eir.at[d], p, c)

    def turn(p):
        @pl.when(p == r)
        def _():
            e_rows[at_row(r), half(k)] = eall[p]

        @pl.when(p != r)
        def _():
            inplane(lax.rem(p - r + R, R) - 1, p).start()

    pair = rc(e_rows.at[:, half(k)], e_rows.at[:, half(k)], ps, pr, r, partner)

    def share(h):
        @pl.when(jnp.logical_or(z - r == h, r - z == h))
        def _():
            for d in range(R - 1):
                inplane(d, rows[d]).wait_recv()
            pair.start()

    def hop(h):
        @pl.when(z - h >= 0)
        def _():
            flow(z - h, 2).wait_recv()

            @pl.when(z < Z - 1)
            def _():
                flow(z - h, 2).start()

        @pl.when(z + h <= Z - 1)
        def _():
            flow(z + h, -2).wait_recv()

            @pl.when(z > 0)
            def _():
                flow(z + h, -2).start()

            turn(z + h)

        @pl.when(z - h >= 0)
        def _():
            turn(z - h)

        share(h - 1)

    def mucopy(d):
        return rc(mbuf.at[c], mbuf.at[c], mus.at[d], mur.at[d], r, cols[d])

    @pl.when(z < Z - 1)
    def _():
        flow(z, 2).start()

    @pl.when(z > 0)
    def _():
        flow(z, -2).start()

    turn(z)
    for d in range(N - 1):
        mucopy(d).start()

    xcopy = rc(xp.at[:, half(1 - k)], xbuf, xs, xr, r, partner)

    def mcopy(d, which):
        q = rows[d]
        return rc(acc.at[which, at_row(q)], mrecv.at[d, which], ms.at[d, which], mrs.at[d, which], q, c)

    def xcopy2(d):
        return rc(xsum.at[at_row(rows[d])], xin.at[r], xis.at[d], xir.at[d], rows[d], c)

    def upcopy(j, col):
        return rc(xin.at[j], up.at[j], ups.at[j], upr.at[j], r, col)

    def x_begin():
        @pl.when(low)
        def _():
            xcopy.start()

    def x_turn():
        @pl.when(low)
        def _():
            xcopy.wait()
            xsum[...] = xp[:, half(k)] + xbuf[...]
            xin[r] = xsum[at_row(r)]
            for d in range(R - 1):
                xcopy2(d).start()

    def climb(zz, j):
        @pl.when(z == zz)
        def _():
            @pl.when(r != j)
            def _():
                d = lax.rem(r - j + R, R)
                rc(xin.at[j], xin.at[j], xis.at[d - 1], xir.at[d - 1], j, c).wait_recv()

            if zz > 0:
                upcopy(j, c - 2).wait_recv()
                xin[j] = xin[j] + up[j]
            if zz < j:
                upcopy(j, c + 2).start()

    def e_ready():
        share(Z - 1)
        pair.wait()

        @pl.loop(0, M // 32)
        def _(i):
            rows32 = pl.ds(pl.multiple_of(i * 32, 32), 32)
            hi, lo = split(e_rows[rows32, :])
            estack[rows32, :] = hi
            estack[pl.ds(pl.multiple_of(M + i * 32, 32), 32), :] = lo

    def m_send(which):
        for d in range(R - 1):
            if which == 0:
                mcopy(d, 0).start()
            else:
                @pl.when(low)
                def _():
                    mcopy(d, 1).start()

    def x_tile(i, slot):
        where = pl.ds(x_start(i), CH)
        xp[:, where] = jnp.zeros((M, CH), F32)

        @pl.loop(0, per)
        def _(b):
            at = pl.ds(pl.multiple_of(b * CH, CH), CH)
            hi, lo = split(tiles[slot, :, at])
            both = dstack[:, at]
            dims = (((1,), (1,)), ((), ()))
            p = lax.dot_general(both, hi, dims, preferred_element_type=F32)
            q = lax.dot_general(both[:M], lo, dims, preferred_element_type=F32)
            xp[:, where] += p[:M] + p[M:] + q

    def m_tile(which, i, slot):
        @pl.loop(0, per)
        def _(b):
            at = pl.ds(pl.multiple_of(b * CH, CH), CH)
            hi, lo = split(tiles[slot, :, at])
            both = estack[:, i * CH : (i + 1) * CH]
            dims = (((1,), (0,)), ((), ()))
            p = lax.dot_general(both, hi, dims, preferred_element_type=F32)
            q = lax.dot_general(both[:M], lo, dims, preferred_element_type=F32)
            out = p[:M] + p[M:] + q
            if i == 0:
                acc[which, :, at] = out
            else:
                acc[which, :, at] += out

    @pl.loop(0, M // 32)
    def _(i):
        rows32 = pl.ds(pl.multiple_of(i * 32, 32), 32)
        old = c_prev[rows32, :]
        hi, lo = split(1.5 * old * old)
        dstack[rows32, :] = hi
        dstack[pl.ds(pl.multiple_of(M + i * 32, 32), 32), :] = lo

    hooks = {}

    def hook(n, f, *args):
        hooks.setdefault(n, []).append((f, args))

    hook(per - 1, x_begin)
    for h in range(1, Z):
        hook(min((h * count) // Z - 1 + (h > 2), count - 1), hop, h)
    hook(count - 1, e_ready)
    hook(count, x_turn)
    for zz in range(Z):
        for j in reversed(range(zz, Z)):
            hook(count + 2 + 2 * zz + (Z - 1 - j), climb, zz, j)
    hook(2 * count - 1, m_send, 0)
    hook(3 * count - 1, m_send, 1)
    for n in range(3 * count):
        if n + 2 < 3 * count:
            tile_copy(n + 2).start()
        tile_copy(n).wait()
        kind, i = divmod(n, count)
        if kind == 0:
            x_tile(i, n % SLOTS)
        else:
            m_tile(kind - 1, i, n % SLOTS)
        for f, args in hooks.get(n, ()):
            f(*args)

    for d in range(N - 1):
        mucopy(d).wait_recv()
    total = mbuf[0]
    for i in range(1, N):
        total = total + mbuf[i]
    scalar = WARMTH + coef * jnp.sum(total, axis=1, keepdims=True)
    racc[0] = acc[0, at_row(r)] + xin[z]
    racc[1] = acc[1, at_row(r)]
    for d in range(R - 1):
        mcopy(d, 0).wait_recv()
        racc[0] = racc[0] + mrecv[d, 0]
    for d in range(R - 1):
        @pl.when(z <= lax.rem(r - d - 1 + R, R))
        def _():
            mcopy(d, 1).wait_recv()
            racc[1] = racc[1] + mrecv[d, 1]

    cn = c_in[...] + STEP * (coef * racc[0] - scalar * c_in[...])
    rn = r_in[...] + STEP * (coef * racc[1] - scalar * r_in[...])
    csrc[0] = cn
    c_full[at_row(r)] = cn
    fulls = [c_full]
    if last:
        csrc[1] = rn
        r_full[at_row(r)] = rn
        fulls.append(r_full)
    else:
        c_out[...] = cn
        r_out[...] = rn

    def gcopy(d, which):
        return rc(csrc.at[which], fulls[which].at[at_row(r)], cs.at[d, which], crs.at[d, which], rows[d], c)

    for which in range(len(fulls)):
        for d in range(R - 1):
            gcopy(d, which).start()
    for d in range(N - 1):
        mucopy(d).wait_send()
    for p in range(Z):
        @pl.when(jnp.logical_and(p <= z, z < Z - 1))
        def _():
            flow(p, 2).wait_send()

        @pl.when(jnp.logical_and(p >= z, z > 0))
        def _():
            flow(p, -2).wait_send()
    for d in range(R - 1):
        inplane(d, rows[d]).wait_send()
        mcopy(d, 0).wait_send()

    @pl.when(low)
    def _():
        for d in range(R - 1):
            mcopy(d, 1).wait_send()
            xcopy2(d).wait_send()
    for j in range(Z):
        @pl.when(z < j)
        def _():
            upcopy(j, c + 2).wait_send()
    for which in range(len(fulls)):
        for d in range(R - 1):
            gcopy(d, which).wait()


def block_call(last, coef, R, Z, hc, hr, c_full, c, r):
    dma, vmem = pltpu.SemaphoreType.DMA, pltpu.VMEM
    T, U = c.shape
    M, N, CH = R * T, 2 * Z, U // 4
    scratch = [
        vmem((SLOTS, CH, U), F32),
        vmem((M, 2 * U), F32),
        vmem((2, M, U), F32),
        vmem((M, 2 * U), F32),
        vmem((2 * M, 2 * U), BF16),
        vmem((2 * M, U), BF16),
        vmem((M, U), F32),
        vmem((M, U), F32),
        vmem((R, T, U), F32),
        vmem((Z, T, U), F32),
        vmem((R - 1, 2, T, U), F32),
        vmem((2, T, U), F32),
        vmem((2, T, U), F32),
        vmem((Z, T, U), F32),
        vmem((N, T, 128), F32),
        dma((SLOTS,)),
    ]
    scratch += [dma, dma, dma((R - 1,)), dma((R - 1,)), dma((Z,)), dma((Z,))] + [dma((R - 1, 2))] * 4
    scratch += [dma((Z,))] * 4 + [dma((R - 1,))] * 2 + [dma, dma] + [dma((N - 1,))] * 2
    piece, full = (T, U), (M, U)
    shapes = (full, full) if last else (piece, piece, full)
    spec, hbm = pl.BlockSpec(memory_space=pltpu.VMEM), pl.BlockSpec(memory_space=pl.ANY)
    return pl.pallas_call(
        functools.partial(block_kernel, last, coef, R, Z),
        out_shape=[jax.ShapeDtypeStruct(s, F32) for s in shapes],
        in_specs=[hbm, hbm, spec, spec, spec],
        out_specs=[spec] * len(shapes),
        scratch_shapes=scratch,
        name="block_last" if last else "block_mid",
        compiler_params=pltpu.CompilerParams(collective_id=2 if last else 1, has_side_effects=True),
    )(hc, hr, c_full, c, r)


def kernel_body(hist_corr, hist_resp, row_corr, row_resp):
    R, N = lax.axis_size("row"), lax.axis_size("col")
    T = row_corr.shape[0] // R
    coef = 1.0 / math.sqrt(hist_corr.shape[0] * R)
    start = lax.axis_index("row") * T
    corr = lax.dynamic_slice_in_dim(row_corr, start, T, 0)
    resp = lax.dynamic_slice_in_dim(row_resp, start, T, 0)
    full = row_corr
    for _ in range(BLOCKS - 1):
        corr, resp, full = block_call(False, coef, R, N // 2, hist_corr, hist_resp, full, corr, resp)
    return tuple(block_call(True, coef, R, N // 2, hist_corr, hist_resp, full, corr, resp))


def solution(mesh):
    R, N = mesh.shape["row"], mesh.shape["col"]
    body = kernel_body if N == 2 * R and R == 4 else plain_body
    in_specs = (P("row", "col"), P("row", "col"), P(None, "col"), P(None, "col"))
    out_specs = (P(None, "col"), P(None, "col"))
    return jax.shard_map(body, mesh=mesh, in_specs=in_specs, out_specs=out_specs, check_vma=False)
```
